128 devices in a mesh: img: 16 (over x_hi, y, core), pose: 8 (over z, x_lo).
Axes of the slice: x: 4 (x_hi: 2, x_lo: 2; x = x_hi * 2 + x_lo), y: 4, z: 4, core: 2. Of those that a mesh axis runs over, the one named last changes fastest.
Arguments:
- images: bfloat16 [2048, 8192], P('img'), may hold values from -240 to 240
- shift_phase: float32 [8, 4096], replicated, may hold values from -3.140625 to 3.140625
- noise_weight: float32 [8192], replicated, may hold values from 0.005 to 0.05
- refs: bfloat16 [3072, 8192], P('pose', 'img'), may hold values from -6 to 6
- routing: int32 [98304, 1], P(('pose', 'img')), may hold values from 0 to 127; in each aligned block of 768 rows (0 to 767, 768 to 1535, ...) at most 12 rows name the same one
- stencil: int32 [98304], P(('pose', 'img')), may hold values from 0 to 7
- interp: bfloat16 [128, 8, 256, 512], P(('img', 'pose')), may hold values from -48 to 48
Outputs:
- volume: float32 [128, 512], P(('img', 'pose'))
- evidence: float32 [2048], P('img')
The draws below stay inside these ranges and needn't reach their ends.
Inputs may be any that keep to these rules, and one draw needn't show every extreme that they name: `routing`: among the rows of one device no brick is named more than 12 times, a bound that some block reaches there.
All inputs are finite; a program needn't handle non-finite values.
Results may differ from the reference program's by a relative error of at most 0.0052.
Values may be sent and summed in bfloat16 or wider, within the bound.
No kernel may reach another device: no remote copies, remote signals or barrier semaphores. Data moves between devices by JAX's collectives and lax.ppermute only.
A program may use at most 192 MiB of HBM per device.

```python
import math
import jax
import jax.numpy as jnp
import numpy as np
from jax import lax

PIX = 4096
TRANS = 8
BLOCK = 128
STENCILS = 8
CELLS = 512
IMGS = 2048
POSES = 3072
NBLK = 32
BRICKS = 128
CAP = 12
DEVICES = 128


def draw_images(key, part):
    first_key = jax.random.fold_in(jax.random.fold_in(key, 11), 0)
    values = jnp.clip(jax.random.normal(first_key, (IMGS, 2 * PIX), jnp.float32), -6.0, 6.0)
    return values.astype(jnp.bfloat16)


def draw_refs(key, part):
    first_key = jax.random.fold_in(jax.random.fold_in(key, 23), 0)
    values = jnp.clip(jax.random.normal(first_key, (POSES, 2 * PIX), jnp.float32), -6.0, 6.0)
    return values.astype(jnp.bfloat16)


def with_ends(entries, stream_key, least, high):
    spot = [jax.random.randint(jax.random.fold_in(stream_key, axis), (), 0, length) for axis, length in enumerate(entries.shape)]
    widest = entries.shape.index(max(entries.shape))
    next_to = spot[:widest] + [(spot[widest] + 1) % entries.shape[widest]] + spot[widest + 1:]
    return entries.at[tuple(spot)].set(least).at[tuple(next_to)].set(high)


def levels(key, dims, pieces, least, largest):
    def one(axis_at, parts):
        heights = jax.random.uniform(jax.random.fold_in(jax.random.fold_in(key, 6), axis_at), (parts,), jnp.float32, least / len(pieces), largest / len(pieces))
        return jnp.repeat(jnp.exp(heights), dims[axis_at] // parts).reshape((-1,) + (1,) * (len(dims) - axis_at - 1))

    loudness = one(*pieces[0])
    for cut in pieces[1:]:
        loudness = loudness * one(*cut)
    return loudness


def routed_block(own_key, own, number, rows, amount, top, reach, lean):
    sequence = jax.random.permutation(own_key, amount)
    heavy_load, ordinary = portions_of(amount, rows * top, reach, lean, True), portions_of(amount, rows * top, reach, lean, False)
    places = jnp.arange(amount)

    def named(sizes, rotation):
        used = int((sizes > 0).sum())
        fixed = max(1, used // 4)
        passed = fixed + (places - fixed + rotation * (used - fixed)) % max(1, amount - fixed)
        return jnp.zeros((amount,), jnp.int32).at[sequence[jnp.where(places < fixed, places, passed)]].set(jnp.asarray(sizes, jnp.int32))

    sizes = jnp.where(number % 4 == 0, named(heavy_load, number // 4), named(ordinary, number - number // 4 - 1))
    mixed = jax.random.permutation(jax.random.fold_in(own, 3), amount)
    donor, taker = mixed[0:amount // 2 * 2:2], mixed[1:amount // 2 * 2:2]
    room = jnp.minimum(sizes[donor] - 1, reach - sizes[taker]) // 2
    room = jnp.where((donor == sequence[0]) | (taker == sequence[0]) | (sizes[taker] == 0), 0, jnp.maximum(room, 0))
    passed = jax.random.randint(jax.random.fold_in(own, 4), (amount // 2,), 0, 1 << 20) % (room + 1)
    sizes = sizes.at[donor].add(-passed).at[taker].add(passed)
    members = jnp.searchsorted(jnp.cumsum(sizes), jnp.arange(rows * top), side="right").astype(jnp.int32)
    grid = members.reshape(top, rows).T
    grid = grid[jax.random.permutation(jax.random.fold_in(own, 1), rows)]
    rotation = jax.random.randint(jax.random.fold_in(own, 2), (rows, 1), 0, top)
    return jnp.take_along_axis(grid, (jnp.arange(top)[None, :] + rotation) % top, axis=1)


def portions_of(amount, total, most, slope, full):
    loads = [(1 << 20) // math.isqrt(standing ** slope) + 1 for standing in range(1, amount + 1)]
    largest = most if full else min(most, max(-(-total // amount), total * loads[0] // sum(loads)))
    least = 1 if total - largest >= amount - 1 else 0
    given, rest = [largest] + [least] * (amount - 1), total - largest - least * (amount - 1)
    while rest > 0:
        candidates = [i for i in range(1, amount) if given[i] < largest] or [i for i in range(1, amount) if given[i] < most]
        whole, budget = sum([loads[i] for i in candidates]), rest
        for i in candidates:
            more = min(most - given[i], max(1, budget * loads[i] // whole), rest)
            given[i] = given[i] + more
            rest = rest - more
    return np.array(given)


def scatter_about(key, shape, spread, bound, cuts=(), held_as=jnp.bfloat16):
    array = spread * jax.random.normal(key, shape, jnp.float32)
    if cuts:
        array = array * levels(key, shape, cuts, -0.22, 0.18)
    return jnp.clip(array, -bound, bound).astype(held_as)


def setup_inputs(seed: int = 0) -> dict:
    streams_of = jax.random.split(jax.random.key(seed), 8)
    images = draw_images(jax.random.fold_in(streams_of[7], 71), 0)
    shift_phase = jnp.clip(jax.random.uniform(streams_of[1], (TRANS, PIX), jnp.float32, -3.140625, 3.140625), -3.140625, 3.140625)
    noise_weight = jnp.clip(jnp.exp(jax.random.uniform(streams_of[2], (2 * PIX,), jnp.float32, math.log(0.005), math.log(0.05))), 0.005, 0.05)
    refs = draw_refs(jax.random.fold_in(streams_of[7], 71), 0)
    routing_keys = jax.random.split(jax.random.fold_in(streams_of[4], 1), (POSES * NBLK) // (POSES * NBLK // DEVICES))
    routing_turns = jax.random.permutation(jax.random.fold_in(streams_of[4], 3), (POSES * NBLK) // (POSES * NBLK // DEVICES))
    routing = jax.vmap(lambda own, number: routed_block(jax.random.fold_in(streams_of[4], 2), own, number, POSES * NBLK // DEVICES, BRICKS, 1, CAP, 2))(routing_keys, routing_turns).reshape((POSES * NBLK, 1))
    stencil = with_ends(jax.random.randint(streams_of[5], (POSES * NBLK,), 0, STENCILS), jax.random.fold_in(streams_of[5], 1), 0, STENCILS - 1).astype(jnp.int32)
    interp = scatter_about(streams_of[6], (BRICKS, STENCILS, 2 * BLOCK, CELLS), 8.0, 48.0, ((0, 128),))
    return dict(images=images, shift_phase=shift_phase, noise_weight=noise_weight, refs=refs, routing=routing, stencil=stencil, interp=interp)


def translated(images, shift_phase, noise_weight):
    count = images.shape[0]
    blocks = images.astype(jnp.float32).reshape(count, 1, PIX // BLOCK, 2, BLOCK)
    real_part = blocks[:, :, :, 0, :]
    imag_part = blocks[:, :, :, 1, :]
    angles = shift_phase.reshape(1, TRANS, PIX // BLOCK, BLOCK)
    cosine = jnp.cos(angles)
    sine = jnp.sin(angles)
    new_real = real_part * cosine + imag_part * sine
    new_imag = imag_part * cosine - real_part * sine
    stacked = jnp.stack([new_real, new_imag], axis=3).reshape(count * TRANS, 2 * PIX)
    return (stacked * noise_weight[None, :]).astype(jnp.bfloat16)

def brick_volume(pair):
    gathered_row, matrices = pair
    flat = matrices.reshape(STENCILS * 2 * BLOCK, CELLS)
    return jnp.dot(gathered_row[None, :], flat, preferred_element_type=jnp.float32)[0]

def reference(images, shift_phase, noise_weight, refs, routing, stencil, interp):
    weighted = translated(images, shift_phase, noise_weight)
    refs_wide = refs.astype(jnp.float32)
    half_norm = 0.5 * lax.optimization_barrier(jnp.sum(refs_wide * refs_wide * noise_weight[None, :], axis=1))
    scores = lax.dot_general(weighted, refs, (((1,), (1,)), ((), ())), preferred_element_type=jnp.float32)
    scores = scores - half_norm[None, :]
    grouped = scores.reshape(IMGS, TRANS * POSES)
    peak = lax.optimization_barrier(jnp.max(grouped, axis=1))
    expo = jnp.exp(grouped - peak[:, None])
    total = lax.optimization_barrier(jnp.sum(expo, axis=1))
    evidence = peak + jnp.log(total)
    posterior = (expo / total[:, None]).astype(jnp.bfloat16).reshape(IMGS * TRANS, POSES)
    accum = lax.dot_general(posterior, weighted, (((0,), (0,)), ((), ())), preferred_element_type=jnp.float32)
    block_rows = accum.astype(jnp.bfloat16).reshape(POSES * NBLK, 2 * BLOCK)
    target = routing[:, 0].astype(jnp.int32)
    segment_ids = (target * STENCILS + stencil).astype(jnp.int32)
    gathered = jax.ops.segment_sum(block_rows.astype(jnp.float32), segment_ids, num_segments=BRICKS * STENCILS)
    gathered = gathered.astype(jnp.bfloat16).reshape(BRICKS, STENCILS * 2 * BLOCK)
    summed = lax.map(brick_volume, (gathered, interp))
    counts = jax.ops.segment_sum(jnp.ones((POSES * NBLK,), jnp.float32), target, num_segments=BRICKS)
    volume = summed * lax.rsqrt(1.0 + counts)[:, None]
    return (volume, evidence)
```

```python
import jax
import jax.numpy as jnp
from jax import lax
from jax.experimental import pallas as pl
from jax.experimental.pallas import tpu as pltpu
from jax.sharding import Mesh
from jax.sharding import PartitionSpec as P

PIX = 4096
TRANS = 8
BLOCK = 128
STENCILS = 8
NBLK = 32
BRICKS = 128
CELLS = 512
SLICE = 512
IMG = ("xh", "y", "c")
POSE = ("z", "xl")
IMG_POSE = ("xh", "y", "c", "z", "xl")
POSE_IMG = ("z", "xl", "xh", "y", "c")
F32 = jnp.float32
BF16 = jnp.bfloat16


def weight_kernel(img, cos, sin, out):
    x = img[...].astype(F32)
    n = x.shape[0]
    parts = []
    for b in range(x.shape[1] // 256):
        parts.append(x[:, b * 256 + 128 : b * 256 + 256])
        parts.append(x[:, b * 256 : b * 256 + 128])
    swapped = jnp.concatenate(parts, axis=1)
    for t in range(TRANS):
        w = x * cos[t : t + 1, :] + swapped * sin[t : t + 1, :]
        out[t * n : (t + 1) * n, :] = w.astype(BF16)


def weight_rows(images, cos, sin):
    n, width = images.shape
    step = 512
    return pl.pallas_call(
        weight_kernel,
        grid=(width // step,),
        in_specs=[
            pl.BlockSpec((n, step), lambda i: (0, i)),
            pl.BlockSpec((TRANS, step), lambda i: (0, i)),
            pl.BlockSpec((TRANS, step), lambda i: (0, i)),
        ],
        out_specs=pl.BlockSpec((n * TRANS, step), lambda i: (0, i)),
        out_shape=jax.ShapeDtypeStruct((n * TRANS, width), BF16),
        name="weigh",
    )(images, cos, sin)


def scores_call(chunks, index, weighted, noise, carried, last):
    count = len(chunks)
    arrays = [c[0] for c in chunks]
    offsets = [c[1] for c in chunks]
    rows = weighted.shape[0]
    imgs = rows // TRANS
    poses = 384

    def kernel(idx, *refs):
        del idx
        parts = refs[:count]
        w, nz = refs[count : count + 2]
        rest = refs[count + 2 :]
        if carried is not None:
            s_in, p_in = rest[:2]
            rest = rest[2:]
        if last:
            e_out, st_out, s_acc, p_acc = rest
        else:
            s_acc, p_acc = rest
        step = pl.program_id(0)

        @pl.when(step == 0)
        def _():
            if carried is None:
                s_acc[...] = jnp.zeros(s_acc.shape, F32)
                p_acc[...] = jnp.zeros(p_acc.shape, F32)
            else:
                s_acc[...] = s_in[...]
                p_acc[...] = p_in[...]

        for j in range(count):

            @pl.when(step == j)
            def _(j=j):
                a = parts[j][...]
                lo, n = offsets[j], a.shape[0]
                s_acc[lo : lo + n, :] += lax.dot_general(
                    a, w[...], (((1,), (1,)), ((), ())), preferred_element_type=F32
                )
                wide = a.astype(F32)
                q = wide * wide * nz[...]
                p_acc[lo : lo + n, :] += (
                    q[:, :128] + q[:, 128:256] + (q[:, 256:384] + q[:, 384:])
                )

        if last:

            @pl.when(step == count - 1)
            def _():
                half = 0.5 * jnp.sum(p_acc[...], axis=1, keepdims=True)
                s_acc[...] = s_acc[...] - half
                m = jnp.max(s_acc[...], axis=0, keepdims=True)
                top = m[:, :imgs]
                for t in range(1, TRANS):
                    top = jnp.maximum(top, m[:, t * imgs : (t + 1) * imgs])
                total = jnp.zeros((1, imgs), F32)
                for t in range(TRANS):
                    e = jnp.exp(s_acc[:, t * imgs : (t + 1) * imgs] - top)
                    e_out[:, t * imgs : (t + 1) * imgs] = e
                    total = total + jnp.sum(e, axis=0, keepdims=True)
                st_out[0:1, :] = top
                st_out[1:2, :] = total

    def whole(shape):
        return pl.BlockSpec(shape, lambda i, idx: (0,) * len(shape))

    in_specs = [whole(a.shape) for a in arrays]
    in_specs += [
        pl.BlockSpec((rows, SLICE), lambda i, idx: (0, idx[i])),
        pl.BlockSpec((1, SLICE), lambda i, idx: (0, idx[i])),
    ]
    args = [*arrays, weighted, noise]
    acc_shapes = ((poses, rows), (poses, 128))
    if carried is not None:
        in_specs += [whole(s) for s in acc_shapes]
        args += list(carried)
    if last:
        out_shapes = ((poses, rows), (2, imgs))
        scratch = [pltpu.VMEM(s, F32) for s in acc_shapes]
    else:
        out_shapes = acc_shapes
        scratch = []
    return pl.pallas_call(
        kernel,
        grid_spec=pltpu.PrefetchScalarGridSpec(
            num_scalar_prefetch=1,
            grid=(count,),
            in_specs=in_specs,
            out_specs=[whole(s) for s in out_shapes],
            scratch_shapes=scratch,
        ),
        out_shape=[jax.ShapeDtypeStruct(s, F32) for s in out_shapes],
        name="scores",
    )(index, *args)


def gather_kernel(pieces, own, e, w, seg, g_out, ev_out, post, acc):
    step = pl.program_id(0)

    @pl.when(step == 0)
    def _():
        imgs = own.shape[1]
        peak = pieces[0, 0:1, :]
        for j in range(1, pieces.shape[0]):
            peak = jnp.maximum(peak, pieces[j, 0:1, :])
        total = jnp.zeros_like(peak)
        for j in range(pieces.shape[0]):
            total = total + pieces[j, 1:2, :] * jnp.exp(pieces[j, 0:1, :] - peak)
        ev_out[...] = peak + jnp.log(total)
        scale = jnp.exp(own[0:1, :] - peak) / total
        for t in range(TRANS):
            at = slice(t * imgs, (t + 1) * imgs)
            post[:, at] = (e[:, at] * scale).astype(BF16)
        acc[...] = jnp.zeros(acc.shape, F32)

    rows = jnp.dot(post[...], w[...], preferred_element_type=F32).astype(BF16)
    both = jnp.concatenate([rows[:, :256], rows[:, 256:]], axis=0)
    ids = seg[0]
    hot = lax.broadcasted_iota(jnp.int32, (acc.shape[0], ids.shape[1]), 0) == ids
    hot = jnp.where(hot, 1.0, 0.0).astype(BF16)
    acc[...] += jnp.dot(hot, both, preferred_element_type=F32)

    @pl.when(step == pl.num_programs(0) - 1)
    def _():
        g_out[...] = acc[...].astype(BF16)


def gather_call(pieces, own, e, weighted, seg):
    rows = weighted.shape[0]
    imgs = own.shape[1]
    segs = BRICKS * STENCILS
    return pl.pallas_call(
        gather_kernel,
        grid=(NBLK // 2,),
        in_specs=[
            pl.BlockSpec(pieces.shape, lambda i: (0, 0, 0)),
            pl.BlockSpec(own.shape, lambda i: (0, 0)),
            pl.BlockSpec(e.shape, lambda i: (0, 0)),
            pl.BlockSpec((rows, 512), lambda i: (0, i)),
            pl.BlockSpec((1, 1, seg.shape[2]), lambda i: (i, 0, 0)),
        ],
        out_specs=[
            pl.BlockSpec((segs, 256), lambda i: (0, 0)),
            pl.BlockSpec((1, imgs), lambda i: (0, 0)),
        ],
        out_shape=[
            jax.ShapeDtypeStruct((segs, 256), BF16),
            jax.ShapeDtypeStruct((1, imgs), F32),
        ],
        scratch_shapes=[pltpu.VMEM(e.shape, BF16), pltpu.VMEM((segs, 256), F32)],
        name="gather",
    )(pieces, own, e, weighted, seg)


def volume_kernel(got, interp, count, out):
    total = got[0].astype(F32)
    for j in range(1, got.shape[0]):
        total = total + got[j].astype(F32)
    mixed = total.astype(BF16)
    acc = jnp.zeros((STENCILS, CELLS), F32)
    for s in range(STENCILS):
        row = lax.broadcasted_iota(jnp.int32, mixed.shape, 0) == s
        only = jnp.where(row, total, 0.0).astype(BF16)
        acc = acc + jnp.dot(only, interp[0, s], preferred_element_type=F32)
    del mixed
    out[...] = jnp.sum(acc, axis=0, keepdims=True) * lax.rsqrt(1.0 + count[...])


def volume_call(got, interp, count):
    return pl.pallas_call(
        volume_kernel,
        out_shape=jax.ShapeDtypeStruct((1, CELLS), F32),
        name="volume",
    )(got, interp, count)


def shifted(x, axis, by):
    size = lax.axis_size(axis)
    return lax.ppermute(x, axis, [(i, (i + by) % size) for i in range(size)])


def flipped(x, axis, bit=1):
    size = lax.axis_size(axis)
    return lax.ppermute(x, axis, [(i, i ^ bit) for i in range(size)])


def doubled(x, axis, bit=1):
    other = flipped(x, axis, bit)
    upper = (lax.axis_index(axis) & bit) != 0
    return jnp.where(
        upper, jnp.concatenate([other, x], 0), jnp.concatenate([x, other], 0)
    )


def body(images, shift_phase, noise_weight, refs, routing, stencil, interp):
    xh, y, c = (lax.axis_index(a) for a in IMG)

    def at(fx, dy, fc):
        return (((xh ^ fx) * 4 + (y + dy) % 4) * 2 + (c ^ fc)).astype(jnp.int32)

    near = flipped(refs, "c")
    left = shifted(refs, "y", 1)
    right = shifted(refs, "y", -1)
    across = flipped(refs, "xh")
    low = slice(0, 192)
    high = slice(192, 384)
    far_low = shifted(left[low], "y", 1)
    far_high = shifted(right[high], "y", -1)
    aleft = shifted(across, "y", 1)
    aright = shifted(across, "y", -1)
    afar_low = shifted(aleft[low], "y", 1)
    afar_high = shifted(aright[high], "y", -1)
    place = [
        (refs, 0, (0, 0)),
        (left, 0, (0, -1)),
        (right, 0, (0, 1)),
        (across, 0, (1, 0)),
        (far_low, 0, (0, 2)),
        (far_high, 192, (0, 2)),
        (aleft, 0, (1, -1)),
        (aright, 0, (1, 1)),
        (afar_low, 0, (1, 2)),
        (afar_high, 192, (1, 2)),
    ]

    ids = (routing[:, 0] * STENCILS + stencil).reshape(1, 6, 128)
    ids = doubled(ids, "c")
    ids = doubled(ids, "xh")
    ids = doubled(ids, "y", 1)
    ids = doubled(ids, "y", 2)
    ids = ids.reshape(2, 2, 2, 2, 24, NBLK).transpose(2, 0, 1, 3, 4, 5).reshape(384, NBLK)
    counts = jnp.sum(
        (ids.reshape(1, -1) // STENCILS == jnp.arange(BRICKS, dtype=jnp.int32)[:, None]).astype(F32),
        axis=1,
    )
    seg = ids.T.reshape(NBLK // 2, 1, 768)

    noise = noise_weight.reshape(1, -1)
    by_block = noise_weight.reshape(1, NBLK, 2, BLOCK)
    angles = shift_phase.reshape(TRANS, NBLK, 1, BLOCK)
    cos = (jnp.cos(angles) * by_block).reshape(TRANS, 2 * PIX)
    sign = jnp.array([1.0, -1.0], F32).reshape(1, 1, 2, 1)
    sin = (jnp.sin(angles) * by_block * sign).reshape(TRANS, 2 * PIX)
    weighted = weight_rows(images, cos, sin)

    def group(picks):
        chunks = [(a, lo) for a, lo, _, _ in picks]
        index = jnp.stack([at(f[0], f[1], core) for _, _, f, core in picks])
        return chunks, index

    def mine(js):
        return [(*place[j], 0) for j in js]

    def theirs(js):
        return [(flipped(place[j][0], "c"), *place[j][1:], 1) for j in js]

    first = mine([0]) + [(near, 0, (0, 0), 1)]
    second = mine([1, 2, 3])
    third = theirs([1, 2, 3])
    fourth = mine([4, 5, 6, 7])
    fifth = theirs([4, 5, 6, 7]) + mine([8, 9]) + theirs([8, 9])
    carried = None
    turns = [first, second, third, fourth, fifth]
    for j, picks in enumerate(turns):
        chunks, index = group(picks)
        carried = scores_call(chunks, index, weighted, noise, carried, j == len(turns) - 1)
    e, own = carried

    sent = jnp.concatenate([own, counts.reshape(1, BRICKS)], axis=0)
    pieces = lax.all_to_all(
        jnp.broadcast_to(sent[None], (8, *sent.shape)), POSE, 0, 0, tiled=True
    )
    gathered, evidence = gather_call(pieces, own, e, weighted, seg)
    got = lax.all_to_all(
        gathered.reshape(BRICKS, STENCILS, 2 * BLOCK), IMG_POSE, 0, 0, tiled=True
    )
    brick = lax.axis_index(IMG_POSE)
    count = lax.dynamic_slice(jnp.sum(pieces[:, 2, :], axis=0), (brick,), (1,))
    volume = volume_call(got, interp, count.reshape(1, 1))
    return (volume, evidence.reshape(-1))


def solution(mesh):
    finer = Mesh(mesh.devices.reshape(2, 4, 2, 4, 2), ("xh", "y", "c", "z", "xl"))
    return jax.shard_map(
        body,
        mesh=finer,
        in_specs=(
            P(IMG, None),
            P(),
            P(),
            P(POSE, IMG),
            P(POSE_IMG, None),
            P(POSE_IMG),
            P(IMG_POSE, None, None, None),
        ),
        out_specs=(P(IMG_POSE, None), P(IMG)),
        check_vma=False,
    )
```

```python
import jax
import jax.numpy as jnp
from jax import lax
from jax.experimental import pallas as pl
from jax.experimental.pallas import tpu as pltpu
from jax.sharding import Mesh
from jax.sharding import PartitionSpec as P

PIX = 4096
TRANS = 8
BLOCK = 128
STENCILS = 8
NBLK = 32
BRICKS = 128
CELLS = 512
SLICE = 512
IMG = ("xh", "y", "c")
POSE = ("z", "xl")
IMG_POSE = ("xh", "y", "c", "z", "xl")
POSE_IMG = ("z", "xl", "xh", "y", "c")
F32 = jnp.float32
BF16 = jnp.bfloat16


LIMIT = pltpu.CompilerParams(vmem_limit_bytes=24 << 20)
IDS = 16


def weight_kernel(img, cos, sin, out):
    step = pl.program_id(0)
    n = img.shape[0]
    for p in range(SLICE // 256):
        re_at = slice(p * 256, p * 256 + 128)
        im_at = slice(p * 256 + 128, p * 256 + 256)
        for g in range(0, n, 16):
            re = img[g : g + 16, re_at].astype(F32)
            im = img[g : g + 16, im_at].astype(F32)
            for t in range(TRANS):
                rows = slice(t * n + g, t * n + g + 16)
                new_re = re * cos[t : t + 1, re_at] + im * sin[t : t + 1, re_at]
                new_im = im * cos[t : t + 1, im_at] + re * sin[t : t + 1, im_at]
                out[step, rows, re_at] = new_re.astype(BF16)
                out[step, rows, im_at] = new_im.astype(BF16)


def weight_rows(images, cos, sin):
    n, width = images.shape
    slices = width // SLICE
    return pl.pallas_call(
        weight_kernel,
        grid=(slices,),
        in_specs=[
            pl.BlockSpec((n, SLICE), lambda i: (0, i)),
            pl.BlockSpec((TRANS, SLICE), lambda i: (0, i)),
            pl.BlockSpec((TRANS, SLICE), lambda i: (0, i)),
        ],
        out_specs=pl.BlockSpec(memory_space=pltpu.VMEM),
        out_shape=pltpu.VMEM((slices, n * TRANS, SLICE), BF16),
        compiler_params=LIMIT,
        cost_estimate=pl.CostEstimate(flops=0, bytes_accessed=16 << 20, transcendentals=0),
        name="weigh",
    )(images, cos, sin)


def scores_call(pairs, where, weighted, noise, carried, last):
    count = len(pairs)
    arrays = [a for pair in pairs for a in pair[:2]]
    rows = weighted.shape[1]
    imgs = rows // TRANS
    poses = 384

    def kernel(pos, *refs):
        parts = refs[: 2 * count]
        w, nz = refs[2 * count : 2 * count + 2]
        rest = refs[2 * count + 2 :]
        if carried is not None:
            s_in, p_in, n_in = rest[:3]
            rest = rest[4:]
        if last:
            h_acc, e_out, st_out, s_acc, p_acc = rest
        else:
            s_acc, p_acc, n_acc, h_acc = rest
        number = jnp.zeros((1, BRICKS), F32) if carried is None else n_in[...]
        for j, (_, _, lo, n, (fx, dy)) in enumerate(pairs):
            chip = jnp.bitwise_xor(pos[0], fx) * 4 + jnp.bitwise_and(pos[1] + dy + 4, 3)
            total = None
            norm = None
            for side in range(2):
                at = chip * 2 + jnp.bitwise_xor(pos[2], side)
                a = parts[2 * j + side][:n, :]
                if lo + n == poses:
                    tag = parts[2 * j + side][n : n + IDS, :].astype(F32)
                    number = number + tag[3:4, :BRICKS]
                    for u in range(12):
                        lanes = slice(u % 4 * 128, u % 4 * 128 + 128)
                        h_acc[u, pl.ds(at, 1), :] = tag[u // 4 : u // 4 + 1, lanes]
                d = lax.dot_general(
                    a, w[at], (((1,), (1,)), ((), ())), preferred_element_type=F32
                )
                wide = a.astype(F32)
                q = wide * wide * nz[at]
                q = q[:, :128] + q[:, 128:256] + (q[:, 256:384] + q[:, 384:])
                total = d if total is None else total + d
                norm = q if norm is None else norm + q
            at = slice(lo, lo + n)
            if carried is None:
                s_acc[at, :] = total
                p_acc[at, :] = norm
            else:
                s_acc[at, :] = s_in[at, :] + total
                p_acc[at, :] = p_in[at, :] + norm
        if not last:
            n_acc[...] = number
        if last:
            half = 0.5 * jnp.sum(p_acc[...], axis=1, keepdims=True)
            m = None
            for t in range(TRANS):
                at = slice(t * imgs, (t + 1) * imgs)
                s = s_acc[:, at] - half
                s_acc[:, at] = s
                s = jnp.max(s, axis=0, keepdims=True)
                m = s if m is None else jnp.maximum(m, s)
            total = jnp.zeros((1, imgs), F32)
            for t in range(TRANS):
                at = slice(t * imgs, (t + 1) * imgs)
                e = jnp.exp(s_acc[:, at] - m)
                e_out[:, at] = e
                total = total + jnp.sum(e, axis=0, keepdims=True)
            st_out[0, 0:1, :] = m
            st_out[0, 1:2, :] = total
            st_out[0, 2:3, :] = number

    vmem = pl.BlockSpec(memory_space=pltpu.VMEM)
    smem = pl.BlockSpec(memory_space=pltpu.SMEM)
    in_specs = [smem] + [vmem] * (2 * count + 2)
    args = [where, *arrays, weighted, noise]
    acc_shapes = ((poses, rows), (poses, 128), (1, BRICKS), (12, 16, 128))
    alias = {}
    if carried is not None:
        in_specs += [vmem] * 4
        alias = {len(args) + 3: 0} if last else {len(args) + j: j for j in range(4)}
        args += list(carried)
    if last:
        out_shape = [
            pltpu.VMEM(acc_shapes[3], F32),
            pltpu.VMEM((poses, rows), F32),
            jax.ShapeDtypeStruct((1, 3, imgs), F32),
        ]
        scratch = [pltpu.VMEM(s, F32) for s in acc_shapes[:2]]
    else:
        out_shape = [pltpu.VMEM(s, F32) for s in acc_shapes]
        scratch = []
    work = sum(2 * 2 * p[3] * SLICE * rows for p in pairs)
    return pl.pallas_call(
        kernel,
        in_specs=in_specs,
        out_specs=[vmem] * len(out_shape),
        scratch_shapes=scratch,
        out_shape=out_shape,
        input_output_aliases=alias,
        compiler_params=LIMIT,
        cost_estimate=pl.CostEstimate(flops=work, bytes_accessed=1 << 20, transcendentals=0),
        name="scores",
    )(*args)


def route_kernel(h, seg):
    ids = None
    for kind, scale in ((0, STENCILS), (1, 1)):
        flat = h[6 * kind : 6 * kind + 6].reshape(96, 128)
        turned = flat.T.astype(BF16)
        u = lax.broadcasted_iota(jnp.int32, (96, 384), 0)
        pose = (u & 15) * 24 + (u >> 4) * 4
        k = lax.broadcasted_iota(jnp.int32, (96, 384), 1)
        for j in range(4):
            put = jnp.where(k == pose + j, 1.0, 0.0).astype(BF16)
            part = jnp.dot(turned[j * 32 : j * 32 + 32, :], put, preferred_element_type=F32)
            part = part * float(scale)
            ids = part if ids is None else ids + part
    seg[...] = ids.astype(jnp.int32)


def route_call(h):
    return pl.pallas_call(
        route_kernel,
        in_specs=[pl.BlockSpec(memory_space=pltpu.VMEM)],
        out_specs=pl.BlockSpec(memory_space=pltpu.VMEM),
        out_shape=pltpu.VMEM((NBLK, 384), jnp.int32),
        compiler_params=LIMIT,
        cost_estimate=pl.CostEstimate(flops=1 << 26, bytes_accessed=1 << 20, transcendentals=0),
        name="route",
    )(h)


def gather_kernel(pos, pieces, e, w, seg, g_out, ev_out, num_out, post, acc):
    step = pl.program_id(0)

    @pl.when(step == 0)
    def _():
        imgs = pieces.shape[2]
        group = [pieces[jnp.bitwise_xor(pos[3], j)] for j in range(8)]
        peak = group[0][0:1, :]
        for g in group[1:]:
            peak = jnp.maximum(peak, g[0:1, :])
        total = jnp.zeros_like(peak)
        number = jnp.zeros_like(peak)
        for g in group:
            total = total + g[1:2, :] * jnp.exp(g[0:1, :] - peak)
            number = number + g[2:3, :]
        ev_out[...] = peak + jnp.log(total)
        here = lax.broadcasted_iota(jnp.int32, number.shape, 1) == pos[4]
        num_out[...] = jnp.sum(jnp.where(here, number, 0.0), axis=1, keepdims=True)
        scale = jnp.exp(pieces[0, 0:1, :] - peak) / total
        for t in range(TRANS):
            at = slice(t * imgs, (t + 1) * imgs)
            post[:, at] = (e[:, at] * scale).astype(BF16)
        acc[...] = jnp.zeros(acc.shape, F32)

    rows = jnp.dot(post[...], w[step], preferred_element_type=F32).astype(BF16)
    both = jnp.concatenate([rows[:, :256], rows[:, 256:]], axis=0)
    ids = jnp.concatenate([seg[pl.ds(2 * step, 1), :], seg[pl.ds(2 * step + 1, 1), :]], axis=1)
    hot = lax.broadcasted_iota(jnp.int32, (acc.shape[0], ids.shape[1]), 0) == ids
    hot = jnp.where(hot, 1.0, 0.0).astype(BF16)
    acc[...] += jnp.dot(hot, both, preferred_element_type=F32)

    @pl.when(step == pl.num_programs(0) - 1)
    def _():
        g_out[...] = acc[...].astype(BF16)


def gather_call(where, pieces, e, weighted, seg):
    segs = BRICKS * STENCILS
    vmem = pl.BlockSpec(memory_space=pltpu.VMEM)
    return pl.pallas_call(
        gather_kernel,
        grid=(weighted.shape[0],),
        in_specs=[pl.BlockSpec(memory_space=pltpu.SMEM)] + [vmem] * 4,
        out_specs=[vmem] * 3,
        out_shape=[
            jax.ShapeDtypeStruct((segs, 256), BF16),
            jax.ShapeDtypeStruct((1, pieces.shape[2]), F32),
            jax.ShapeDtypeStruct((1, 1), F32),
        ],
        scratch_shapes=[pltpu.VMEM(e.shape, BF16), pltpu.VMEM((segs, 256), F32)],
        compiler_params=LIMIT,
        name="gather",
    )(where, pieces, e, weighted, seg)


def volume_kernel(got, interp, count, out):
    total = got[0].astype(F32)
    for j in range(1, got.shape[0]):
        total = total + got[j].astype(F32)
    mixed = total.astype(BF16)
    acc = jnp.zeros((STENCILS, CELLS), F32)
    for s in range(STENCILS):
        row = lax.broadcasted_iota(jnp.int32, mixed.shape, 0) == s
        only = jnp.where(row, total, 0.0).astype(BF16)
        acc = acc + jnp.dot(only, interp[0, s], preferred_element_type=F32)
    del mixed
    out[...] = jnp.sum(acc, axis=0, keepdims=True) * lax.rsqrt(1.0 + count[...])


def volume_call(got, interp, count):
    return pl.pallas_call(
        volume_kernel,
        out_shape=jax.ShapeDtypeStruct((1, CELLS), F32),
        compiler_params=LIMIT,
        name="volume",
    )(got, interp, count)


def shifted(x, axis, by):
    size = lax.axis_size(axis)
    return lax.ppermute(x, axis, [(i, (i + by) % size) for i in range(size)])


def flipped(x, axis):
    return lax.ppermute(x, axis, [(0, 1), (1, 0)])


def body(images, shift_phase, noise_weight, refs, routing, stencil, interp):
    xh, y, c = (lax.axis_index(a) for a in IMG)

    tags = jnp.concatenate([routing[:, 0], stencil]).astype(BF16).reshape(3, SLICE)
    own_counts = jnp.sum(
        (routing == jnp.arange(BRICKS, dtype=jnp.int32)[None, :]).astype(F32), axis=0, keepdims=True
    ).astype(BF16)
    tags = jnp.concatenate(
        [
            tags,
            jnp.pad(own_counts, ((0, 0), (0, SLICE - BRICKS))),
            jnp.zeros((IDS - 4, SLICE), BF16),
        ]
    )
    mine = jnp.concatenate([refs, tags], axis=0)

    across = flipped(mine, "xh")
    left = shifted(mine, "y", 1)
    right = shifted(mine, "y", -1)
    far_low = shifted(left[:192], "y", 1)
    far_high = shifted(right[192:], "y", -1)
    aleft = shifted(across, "y", 1)
    aright = shifted(across, "y", -1)
    afar_low = shifted(aleft[:192], "y", 1)
    afar_high = shifted(aright[192:], "y", -1)
    rounds = [
        [(mine, 0, 384, (0, 0))],
        [(left, 0, 384, (0, -1)), (right, 0, 384, (0, 1)), (across, 0, 384, (1, 0))],
        [
            (far_low, 0, 192, (0, 2)),
            (far_high, 192, 192, (0, 2)),
            (aleft, 0, 384, (1, -1)),
            (aright, 0, 384, (1, 1)),
        ],
        [(afar_low, 0, 192, (1, 2)), (afar_high, 192, 192, (1, 2))],
    ]

    noise = noise_weight.reshape(16, 1, SLICE)
    by_block = noise_weight.reshape(1, NBLK, 2, BLOCK)
    angles = shift_phase.reshape(TRANS, NBLK, 1, BLOCK)
    cos = (jnp.cos(angles) * by_block).reshape(TRANS, 2 * PIX)
    sign = jnp.array([1.0, -1.0], F32).reshape(1, 1, 2, 1)
    sin = (jnp.sin(angles) * by_block * sign).reshape(TRANS, 2 * PIX)
    pose = lax.axis_index(POSE)
    where = jnp.stack([xh, y, c, pose, lax.axis_index(IMG_POSE)]).astype(jnp.int32)
    where, cos = lax.optimization_barrier((where, cos))
    weighted = weight_rows(images, cos, sin)

    paired = [[(p[0], flipped(p[0], "c"), *p[1:]) for p in turn] for turn in rounds]

    carried = None
    for j, pairs in enumerate(paired):
        carried = scores_call(pairs, where, weighted, noise, carried, j == len(paired) - 1)
    marks, e, pieces = carried

    for axis, bit in (("xl", 1), ("z", 1), ("z", 2)):
        size = lax.axis_size(axis)
        other = lax.ppermute(pieces, axis, [(i, i ^ bit) for i in range(size)])
        pieces = jnp.concatenate([pieces, other], axis=0)
    seg = route_call(marks)
    gathered, evidence, count = gather_call(where, pieces, e, weighted, seg)
    got = lax.all_to_all(
        gathered.reshape(BRICKS, STENCILS, 2 * BLOCK), IMG_POSE, 0, 0, tiled=True
    )
    volume = volume_call(got, interp, count)
    return (volume, evidence.reshape(-1))


def solution(mesh):
    finer = Mesh(mesh.devices.reshape(2, 4, 2, 4, 2), ("xh", "y", "c", "z", "xl"))
    return jax.shard_map(
        body,
        mesh=finer,
        in_specs=(
            P(IMG, None),
            P(),
            P(),
            P(POSE, IMG),
            P(POSE_IMG, None),
            P(POSE_IMG),
            P(IMG_POSE, None, None, None),
        ),
        out_specs=(P(IMG_POSE, None), P(IMG)),
        check_vma=False,
    )
```

```python
import jax
import jax.numpy as jnp
from jax import lax
from jax.experimental import pallas as pl
from jax.experimental.pallas import tpu as pltpu
from jax.sharding import Mesh
from jax.sharding import PartitionSpec as P

PIX = 4096
TRANS = 8
BLOCK = 128
STENCILS = 8
NBLK = 32
BRICKS = 128
CELLS = 512
SLICE = 512
IMG = ("xh", "y", "c")
POSE = ("z", "xl")
IMG_POSE = ("xh", "y", "c", "z", "xl")
POSE_IMG = ("z", "xl", "xh", "y", "c")
F32 = jnp.float32
BF16 = jnp.bfloat16


LIMIT = pltpu.CompilerParams(vmem_limit_bytes=24 << 20)
IDS = 16


def weight_kernel(img, cos, sin, out):
    step = pl.program_id(0)
    n = img.shape[0]
    for p in range(SLICE // 256):
        re_at = slice(p * 256, p * 256 + 128)
        im_at = slice(p * 256 + 128, p * 256 + 256)
        for g in range(0, n, 16):
            re = img[g : g + 16, re_at].astype(F32)
            im = img[g : g + 16, im_at].astype(F32)
            for t in range(TRANS):
                rows = slice(t * n + g, t * n + g + 16)
                new_re = re * cos[t : t + 1, re_at] + im * sin[t : t + 1, re_at]
                new_im = im * cos[t : t + 1, im_at] + re * sin[t : t + 1, im_at]
                out[step, rows, re_at] = new_re.astype(BF16)
                out[step, rows, im_at] = new_im.astype(BF16)


def weight_rows(images, cos, sin):
    n, width = images.shape
    slices = width // SLICE
    return pl.pallas_call(
        weight_kernel,
        grid=(slices,),
        in_specs=[
            pl.BlockSpec((n, SLICE), lambda i: (0, i)),
            pl.BlockSpec((TRANS, SLICE), lambda i: (0, i)),
            pl.BlockSpec((TRANS, SLICE), lambda i: (0, i)),
        ],
        out_specs=pl.BlockSpec(memory_space=pltpu.VMEM),
        out_shape=pltpu.VMEM((slices, n * TRANS, SLICE), BF16),
        compiler_params=LIMIT,
        cost_estimate=pl.CostEstimate(flops=0, bytes_accessed=16 << 20, transcendentals=0),
        name="weigh",
    )(images, cos, sin)


def scores_call(pairs, where, weighted, noise, carried, last):
    count = len(pairs)
    arrays = [a for pair in pairs for a in pair[:2]]
    rows = weighted.shape[1]
    imgs = rows // TRANS
    poses = 384

    def kernel(pos, *refs):
        parts = refs[: 2 * count]
        w, nz = refs[2 * count : 2 * count + 2]
        rest = refs[2 * count + 2 :]
        if carried is not None:
            s_in, p_in, n_in = rest[:3]
            rest = rest[4:]
        if last:
            h_acc, e_out, st_out, s_acc, p_acc = rest
        else:
            s_acc, p_acc, n_acc, h_acc = rest
        number = jnp.zeros((1, BRICKS), F32) if carried is None else n_in[...]
        for j, (_, _, lo, n, (fx, dy)) in enumerate(pairs):
            chip = jnp.bitwise_xor(pos[0], fx) * 4 + jnp.bitwise_and(pos[1] + dy + 4, 3)
            total = None
            norm = None
            for side in range(2):
                at = chip * 2 + jnp.bitwise_xor(pos[2], side)
                a = parts[2 * j + side][:n, :]
                if lo + n == poses:
                    tag = parts[2 * j + side][n : n + IDS, :].astype(F32)
                    number = number + tag[3:4, :BRICKS]
                    for u in range(12):
                        lanes = slice(u % 4 * 128, u % 4 * 128 + 128)
                        h_acc[u, pl.ds(at, 1), :] = tag[u // 4 : u // 4 + 1, lanes]
                d = lax.dot_general(
                    a, w[at], (((1,), (1,)), ((), ())), preferred_element_type=F32
                )
                wide = a.astype(F32)
                q = wide * wide * nz[at]
                q = q[:, :128] + q[:, 128:256] + (q[:, 256:384] + q[:, 384:])
                total = d if total is None else total + d
                norm = q if norm is None else norm + q
            at = slice(lo, lo + n)
            if carried is None:
                s_acc[at, :] = total
                p_acc[at, :] = norm
            else:
                s_acc[at, :] = s_in[at, :] + total
                p_acc[at, :] = p_in[at, :] + norm
        if not last:
            n_acc[...] = number
        if last:
            half = 0.5 * jnp.sum(p_acc[...], axis=1, keepdims=True)
            m = None
            for t in range(TRANS):
                at = slice(t * imgs, (t + 1) * imgs)
                s = s_acc[:, at] - half
                s_acc[:, at] = s
                s = jnp.max(s, axis=0, keepdims=True)
                m = s if m is None else jnp.maximum(m, s)
            total = jnp.zeros((1, imgs), F32)
            for t in range(TRANS):
                at = slice(t * imgs, (t + 1) * imgs)
                e = jnp.exp(s_acc[:, at] - m)
                e_out[:, at] = e
                total = total + jnp.sum(e, axis=0, keepdims=True)
            st_out[0, 0:1, :] = m
            st_out[0, 1:2, :] = total
            st_out[0, 2:3, :] = number

    vmem = pl.BlockSpec(memory_space=pltpu.VMEM)
    smem = pl.BlockSpec(memory_space=pltpu.SMEM)
    in_specs = [smem] + [vmem] * (2 * count + 2)
    args = [where, *arrays, weighted, noise]
    acc_shapes = ((poses, rows), (poses, 128), (1, BRICKS), (12, 16, 128))
    alias = {}
    if carried is not None:
        in_specs += [vmem] * 4
        alias = {len(args) + 3: 0} if last else {len(args) + j: j for j in range(4)}
        args += list(carried)
    if last:
        out_shape = [
            pltpu.VMEM(acc_shapes[3], F32),
            pltpu.VMEM((poses, rows), F32),
            jax.ShapeDtypeStruct((1, 3, imgs), F32),
        ]
        scratch = [pltpu.VMEM(s, F32) for s in acc_shapes[:2]]
    else:
        out_shape = [pltpu.VMEM(s, F32) for s in acc_shapes]
        scratch = []
    work = sum(2 * 2 * p[3] * SLICE * rows for p in pairs)
    return pl.pallas_call(
        kernel,
        in_specs=in_specs,
        out_specs=[vmem] * len(out_shape),
        scratch_shapes=scratch,
        out_shape=out_shape,
        input_output_aliases=alias,
        compiler_params=LIMIT,
        cost_estimate=pl.CostEstimate(flops=work, bytes_accessed=1 << 20, transcendentals=0),
        name="scores",
    )(*args)


def route_kernel(h, seg):
    ids = None
    for kind, scale in ((0, STENCILS), (1, 1)):
        flat = h[6 * kind : 6 * kind + 6].reshape(96, 128)
        turned = flat.T.astype(BF16)
        u = lax.broadcasted_iota(jnp.int32, (96, 384), 0)
        pose = (u & 15) * 24 + (u >> 4) * 4
        k = lax.broadcasted_iota(jnp.int32, (96, 384), 1)
        for j in range(4):
            put = jnp.where(k == pose + j, 1.0, 0.0).astype(BF16)
            part = jnp.dot(turned[j * 32 : j * 32 + 32, :], put, preferred_element_type=F32)
            part = part * float(scale)
            ids = part if ids is None else ids + part
    seg[...] = ids.astype(jnp.int32)


def route_call(h):
    return pl.pallas_call(
        route_kernel,
        in_specs=[pl.BlockSpec(memory_space=pltpu.VMEM)],
        out_specs=pl.BlockSpec(memory_space=pltpu.VMEM),
        out_shape=pltpu.VMEM((NBLK, 384), jnp.int32),
        compiler_params=LIMIT,
        cost_estimate=pl.CostEstimate(flops=1 << 26, bytes_accessed=1 << 20, transcendentals=0),
        name="route",
    )(h)


def gather_kernel(pos, pieces, e, w, seg, g_out, ev_out, num_out, post, acc):
    step = pl.program_id(0)

    @pl.when(step == 0)
    def _():
        imgs = pieces.shape[2]
        group = [pieces[jnp.bitwise_xor(pos[3], j)] for j in range(8)]
        peak = group[0][0:1, :]
        for g in group[1:]:
            peak = jnp.maximum(peak, g[0:1, :])
        total = jnp.zeros_like(peak)
        number = jnp.zeros_like(peak)
        for g in group:
            total = total + g[1:2, :] * jnp.exp(g[0:1, :] - peak)
            number = number + g[2:3, :]
        ev_out[...] = peak + jnp.log(total)
        here = lax.broadcasted_iota(jnp.int32, number.shape, 1) == pos[4]
        num_out[...] = jnp.sum(jnp.where(here, number, 0.0), axis=1, keepdims=True)
        scale = jnp.exp(pieces[0, 0:1, :] - peak) / total
        for t in range(TRANS):
            at = slice(t * imgs, (t + 1) * imgs)
            post[:, at] = (e[:, at] * scale).astype(BF16)
        acc[...] = jnp.zeros(acc.shape, F32)

    added = None
    for u in range(2):
        at = 2 * step + u
        rows = jnp.dot(post[...], w[at], preferred_element_type=F32).astype(BF16)
        both = jnp.concatenate([rows[:, :256], rows[:, 256:]], axis=0)
        ids = jnp.concatenate([seg[pl.ds(2 * at, 1), :], seg[pl.ds(2 * at + 1, 1), :]], axis=1)
        hot = lax.broadcasted_iota(jnp.int32, (acc.shape[0], ids.shape[1]), 0) == ids
        hot = jnp.where(hot, 1.0, 0.0).astype(BF16)
        part = jnp.dot(hot, both, preferred_element_type=F32)
        added = part if added is None else added + part
    acc[...] += added

    @pl.when(step == pl.num_programs(0) - 1)
    def _():
        g_out[...] = acc[...].astype(BF16)


def gather_call(where, pieces, e, weighted, seg):
    segs = BRICKS * STENCILS
    vmem = pl.BlockSpec(memory_space=pltpu.VMEM)
    return pl.pallas_call(
        gather_kernel,
        grid=(weighted.shape[0] // 2,),
        in_specs=[pl.BlockSpec(memory_space=pltpu.SMEM)] + [vmem] * 4,
        out_specs=[vmem] * 3,
        out_shape=[
            jax.ShapeDtypeStruct((segs, 256), BF16),
            jax.ShapeDtypeStruct((1, pieces.shape[2]), F32),
            jax.ShapeDtypeStruct((1, 1), F32),
        ],
        scratch_shapes=[pltpu.VMEM(e.shape, BF16), pltpu.VMEM((segs, 256), F32)],
        compiler_params=LIMIT,
        name="gather",
    )(where, pieces, e, weighted, seg)


def volume_kernel(got, interp, count, out):
    total = got[0].astype(F32)
    for j in range(1, got.shape[0]):
        total = total + got[j].astype(F32)
    mixed = total.astype(BF16)
    acc = jnp.zeros((STENCILS, CELLS), F32)
    for s in range(STENCILS):
        row = lax.broadcasted_iota(jnp.int32, mixed.shape, 0) == s
        only = jnp.where(row, total, 0.0).astype(BF16)
        acc = acc + jnp.dot(only, interp[0, s], preferred_element_type=F32)
    del mixed
    out[...] = jnp.sum(acc, axis=0, keepdims=True) * lax.rsqrt(1.0 + count[...])


def volume_call(got, interp, count):
    return pl.pallas_call(
        volume_kernel,
        out_shape=jax.ShapeDtypeStruct((1, CELLS), F32),
        compiler_params=LIMIT,
        name="volume",
    )(got, interp, count)


def shifted(x, axis, by):
    size = lax.axis_size(axis)
    return lax.ppermute(x, axis, [(i, (i + by) % size) for i in range(size)])


def flipped(x, axis):
    return lax.ppermute(x, axis, [(0, 1), (1, 0)])


def body(images, shift_phase, noise_weight, refs, routing, stencil, interp):
    xh, y, c = (lax.axis_index(a) for a in IMG)

    tags = jnp.concatenate([routing[:, 0], stencil]).astype(BF16).reshape(3, SLICE)
    own_counts = jnp.sum(
        (routing == jnp.arange(BRICKS, dtype=jnp.int32)[None, :]).astype(F32), axis=0, keepdims=True
    ).astype(BF16)
    tags = jnp.concatenate(
        [
            tags,
            jnp.pad(own_counts, ((0, 0), (0, SLICE - BRICKS))),
            jnp.zeros((IDS - 4, SLICE), BF16),
        ]
    )
    mine = jnp.concatenate([refs, tags], axis=0)

    noise = noise_weight.reshape(16, 1, SLICE)
    by_block = noise_weight.reshape(1, NBLK, 2, BLOCK)
    angles = shift_phase.reshape(TRANS, NBLK, 1, BLOCK)
    cos = (jnp.cos(angles) * by_block).reshape(TRANS, 2 * PIX)
    sign = jnp.array([1.0, -1.0], F32).reshape(1, 1, 2, 1)
    sin = (jnp.sin(angles) * by_block * sign).reshape(TRANS, 2 * PIX)
    pose = lax.axis_index(POSE)
    where = jnp.stack([xh, y, c, pose, lax.axis_index(IMG_POSE)]).astype(jnp.int32)
    where, cos = lax.optimization_barrier((where, cos))

    def swapped(piece):
        return flipped(piece, "c")

    near = swapped(mine)
    left = shifted(mine, "y", 1)
    right = shifted(mine, "y", -1)
    across = flipped(mine, "xh")
    weighted = weight_rows(images, cos, sin)
    one = scores_call([(mine, near, 0, 384, (0, 0))], where, weighted, noise, None, False)
    left, weighted = lax.optimization_barrier((left, weighted))
    aleft = flipped(left, "xh")
    far = shifted(left, "y", 1)
    aright = shifted(across, "y", -1)

    def pair(piece, flips):
        return (piece, swapped(piece), 0, 384, flips)

    two = scores_call(
        [pair(left, (0, -1)), pair(right, (0, 1)), pair(across, (1, 0))],
        where, weighted, noise, one, False,
    )
    aleft, two = lax.optimization_barrier((aleft, two))
    alow = shifted(aleft[:256], "y", 1)
    ahigh = shifted(aright[256:], "y", -1)
    three = scores_call(
        [pair(far, (0, 2)), pair(aleft, (1, -1))],
        where, weighted, noise, two, False,
    )
    four = scores_call([pair(aright, (1, 1))], where, weighted, noise, three, False)
    alow, ahigh, four = lax.optimization_barrier((alow, ahigh, four))
    low = (alow, swapped(alow), 0, 256, (1, 2))
    high = (ahigh, swapped(ahigh), 256, 128, (1, 2))
    marks, e, pieces = scores_call([low, high], where, weighted, noise, four, True)

    for axis, bit in (("xl", 1), ("z", 1), ("z", 2)):
        size = lax.axis_size(axis)
        other = lax.ppermute(pieces, axis, [(i, i ^ bit) for i in range(size)])
        pieces = jnp.concatenate([pieces, other], axis=0)
    seg = route_call(marks)
    gathered, evidence, count = gather_call(where, pieces, e, weighted, seg)
    got = lax.all_to_all(
        gathered.reshape(BRICKS, STENCILS, 2 * BLOCK), IMG_POSE, 0, 0, tiled=True
    )
    volume = volume_call(got, interp, count)
    return (volume, evidence.reshape(-1))


def solution(mesh):
    finer = Mesh(mesh.devices.reshape(2, 4, 2, 4, 2), ("xh", "y", "c", "z", "xl"))
    return jax.shard_map(
        body,
        mesh=finer,
        in_specs=(
            P(IMG, None),
            P(),
            P(),
            P(POSE, IMG),
            P(POSE_IMG, None),
            P(POSE_IMG),
            P(IMG_POSE, None, None, None),
        ),
        out_specs=(P(IMG_POSE, None), P(IMG)),
        check_vma=False,
    )
```

```python
import jax
import jax.numpy as jnp
from jax import lax
from jax.experimental import pallas as pl
from jax.experimental.pallas import tpu as pltpu
from jax.sharding import Mesh
from jax.sharding import PartitionSpec as P

PIX = 4096
TRANS = 8
BLOCK = 128
STENCILS = 8
NBLK = 32
BRICKS = 128
CELLS = 512
SLICE = 512
IMG = ("xh", "y", "c")
POSE = ("z", "xl")
IMG_POSE = ("xh", "y", "c", "z", "xl")
POSE_IMG = ("z", "xl", "xh", "y", "c")
F32 = jnp.float32
BF16 = jnp.bfloat16


LIMIT = pltpu.CompilerParams(vmem_limit_bytes=12 << 20)
IDS = 8
LOW = 288


def slice_kernel(pos, *arrays):
    sources, out, copied, done = arrays[:4], arrays[4], arrays[5:9], arrays[9]
    copies = [
        pltpu.make_async_copy(sources[j], copied[j], done.at[j]) for j in range(4)
    ]
    for copy in copies:
        copy.start()
    for copy in copies:
        copy.wait()
    refs, noise, routing, stencil = copied
    n = refs.shape[0]
    out[:n, :] = refs[...]
    bricks = routing[...].astype(F32)
    kinds = stencil[...].reshape(1, -1).astype(F32)
    one = bricks[:, :512]
    two = jnp.concatenate([bricks[:, 512:], kinds[:, :256]], axis=1)
    three = kinds[:, 256:]
    lane = lax.broadcasted_iota(jnp.int32, (BRICKS, 128), 0)
    hits = jnp.zeros((BRICKS, 128), F32)
    for u in range(6):
        hits = hits + jnp.where(lane == routing[:, u * 128 : u * 128 + 128], 1.0, 0.0)
    counts = jnp.sum(hits.T, axis=0, keepdims=True)
    chip = pos[0] * 4 + pos[1]
    wide = refs[...].astype(F32)
    q = wide * wide * noise[chip * 2 + pos[2]]
    q = q[:, :128] + q[:, 128:256] + (q[:, 256:384] + q[:, 384:])
    norm = jnp.concatenate(
        [jnp.sum(q[j : j + 128, :].T, axis=0, keepdims=True) for j in range(0, n, 128)], axis=1
    )
    high = norm.astype(BF16).astype(F32)
    four = jnp.concatenate([counts, high], axis=1)
    five = jnp.concatenate([jnp.zeros_like(counts), norm - high], axis=1)
    rest = jnp.zeros((IDS - 5, SLICE), F32)
    tags = jnp.concatenate([one, two, three, four, five, rest], axis=0)
    out[n : n + IDS, :] = tags.astype(BF16)


def slice_call(where, refs, noise, routing, stencil):
    arrays = [
        pltpu.with_memory_space_constraint(a, pltpu.HBM)
        for a in (refs, noise, routing, stencil)
    ]
    return pl.pallas_call(
        slice_kernel,
        in_specs=[pl.BlockSpec(memory_space=pltpu.SMEM)]
        + [pl.BlockSpec(memory_space=pltpu.HBM)] * 4,
        out_specs=pl.BlockSpec(memory_space=pltpu.VMEM),
        scratch_shapes=[pltpu.VMEM(a.shape, a.dtype) for a in arrays]
        + [pltpu.SemaphoreType.DMA((4,))],
        out_shape=jax.ShapeDtypeStruct((refs.shape[0] + IDS, SLICE), BF16),
        compiler_params=LIMIT,
        name="slice",
    )(where, *arrays)


def weight_kernel(img, cos, sin, out, first=0):
    step = first + pl.program_id(0)
    n = img.shape[0]
    for p in range(SLICE // 256):
        re_at = slice(p * 256, p * 256 + 128)
        im_at = slice(p * 256 + 128, p * 256 + 256)
        for g in range(0, n, 16):
            re = img[g : g + 16, re_at].astype(F32)
            im = img[g : g + 16, im_at].astype(F32)
            for t in range(TRANS):
                rows = slice(t * n + g, t * n + g + 16)
                new_re = re * cos[t : t + 1, re_at] + im * sin[t : t + 1, re_at]
                new_im = im * cos[t : t + 1, im_at] + re * sin[t : t + 1, im_at]
                out[step, rows, re_at] = new_re.astype(BF16)
                out[step, rows, im_at] = new_im.astype(BF16)


def weight_rows(images, cos, sin):
    n, width = images.shape
    slices = width // SLICE
    return pl.pallas_call(
        weight_kernel,
        grid=(slices,),
        in_specs=[
            pl.BlockSpec((n, SLICE), lambda i: (0, i)),
            pl.BlockSpec((TRANS, SLICE), lambda i: (0, i)),
            pl.BlockSpec((TRANS, SLICE), lambda i: (0, i)),
        ],
        out_specs=pl.BlockSpec(memory_space=pltpu.VMEM),
        out_shape=pltpu.VMEM((slices, n * TRANS, SLICE), BF16),
        compiler_params=LIMIT,
        cost_estimate=pl.CostEstimate(flops=0, bytes_accessed=16 << 20, transcendentals=0),
        name="weigh",
    )(images, cos, sin)


def weight_half(where, images, cos, sin, turn, filled=None):
    n, width = images.shape
    slices = width // SLICE // 2
    first = turn * slices // 2

    def kernel(pos, img, cos, sin, *rest):
        weight_kernel(img, cos, sin, rest[-1], first)

    def at(i, pos):
        return (0, pos[2] * slices + first + i)

    specs = [
        pl.BlockSpec((n, SLICE), at),
        pl.BlockSpec((TRANS, SLICE), at),
        pl.BlockSpec((TRANS, SLICE), at),
    ]
    args = [where, images, cos, sin]
    vmem = pl.BlockSpec(memory_space=pltpu.VMEM)
    if filled is not None:
        specs.append(vmem)
        args.append(filled)
    return pl.pallas_call(
        kernel,
        grid_spec=pltpu.PrefetchScalarGridSpec(
            num_scalar_prefetch=1, grid=(slices // 2,), in_specs=specs, out_specs=vmem
        ),
        out_shape=pltpu.VMEM((slices, n * TRANS, SLICE), BF16),
        input_output_aliases={} if filled is None else {4: 0},
        compiler_params=LIMIT,
        cost_estimate=pl.CostEstimate(flops=0, bytes_accessed=4 << 20, transcendentals=0),
        name="weigh_half",
    )(*args)


def scores_call(pairs, where, weighted, carried, last):
    arrays = [a for pair in pairs for a in pair[:2] if a is not None]
    count = len(arrays)
    rows = weighted.shape[1]
    imgs = rows // TRANS
    poses = 384

    def kernel(pos, *refs):
        parts = list(refs[:count])
        w = refs[count]
        rest = refs[count + 1 :]
        if carried is not None:
            s_in, p_in, n_in = rest[:3]
            rest = rest[4:]
        if last:
            h_acc, e_out, st_out, s_acc = rest
        else:
            s_acc, p_acc, n_acc, h_acc = rest
        number = jnp.zeros((1, BRICKS), F32) if carried is None else n_in[...]
        norm = jnp.zeros((1, poses), F32) if carried is None else p_in[...]
        for *both, lo, n, (fx, dy) in pairs:
            chip = jnp.bitwise_xor(pos[0], fx) * 4 + jnp.bitwise_and(pos[1] + dy + 4, 3)
            total = None
            for side in range(2):
                if both[side] is None:
                    continue
                part = parts.pop(0)
                at = chip * 2 + jnp.bitwise_xor(pos[2], side)
                a = part[:n, :]
                if lo + n == poses:
                    tag = part[n : n + IDS, :].astype(F32)
                    number = number + tag[3:4, :BRICKS]
                    norm = norm + (tag[3:4, BRICKS:] + tag[4:5, BRICKS:])
                    for u in range(12):
                        lanes = slice(u % 4 * 128, u % 4 * 128 + 128)
                        h_acc[u, pl.ds(at, 1), :] = tag[u // 4 : u // 4 + 1, lanes]
                d = lax.dot_general(
                    a, w[at], (((1,), (1,)), ((), ())), preferred_element_type=F32
                )
                total = d if total is None else total + d
            at = slice(lo, lo + n)
            if carried is None:
                s_acc[at, :] = total
            else:
                s_acc[at, :] = s_in[at, :] + total
        if not last:
            n_acc[...] = number
            p_acc[...] = norm
        if last:
            half = jnp.broadcast_to(0.5 * norm, (8, poses)).T[:, :1]
            m = None
            for t in range(TRANS):
                at = slice(t * imgs, (t + 1) * imgs)
                s = s_acc[:, at] - half
                s_acc[:, at] = s
                s = jnp.max(s, axis=0, keepdims=True)
                m = s if m is None else jnp.maximum(m, s)
            total = jnp.zeros((1, imgs), F32)
            for t in range(TRANS):
                at = slice(t * imgs, (t + 1) * imgs)
                e = jnp.exp(s_acc[:, at] - m)
                e_out[:, at] = e
                total = total + jnp.sum(e, axis=0, keepdims=True)
            st_out[0, 0:1, :] = m
            st_out[0, 1:2, :] = total
            st_out[0, 2:3, :] = number

    vmem = pl.BlockSpec(memory_space=pltpu.VMEM)
    smem = pl.BlockSpec(memory_space=pltpu.SMEM)
    in_specs = [smem] + [vmem] * (count + 1)
    args = [where, *arrays, weighted]
    acc_shapes = ((poses, rows), (1, poses), (1, BRICKS), (12, 16, 128))
    alias = {}
    if carried is not None:
        in_specs += [vmem] * 4
        alias = {len(args) + 3: 0} if last else {len(args) + j: j for j in range(4)}
        args += list(carried)
    if last:
        out_shape = [
            pltpu.VMEM(acc_shapes[3], F32),
            pltpu.VMEM((poses, rows), F32),
            jax.ShapeDtypeStruct((1, 3, imgs), F32),
        ]
        scratch = [pltpu.VMEM(acc_shapes[0], F32)]
    else:
        out_shape = [pltpu.VMEM(s, F32) for s in acc_shapes]
        scratch = []
    work = sum(2 * 2 * p[3] * SLICE * rows for p in pairs)
    return pl.pallas_call(
        kernel,
        in_specs=in_specs,
        out_specs=[vmem] * len(out_shape),
        scratch_shapes=scratch,
        out_shape=out_shape,
        input_output_aliases=alias,
        compiler_params=LIMIT,
        cost_estimate=pl.CostEstimate(flops=work, bytes_accessed=1 << 20, transcendentals=0),
        name="scores",
    )(*args)


def route_kernel(h, seg):
    ids = None
    for kind, scale in ((0, STENCILS), (1, 1)):
        flat = h[6 * kind : 6 * kind + 6].reshape(96, 128)
        turned = flat.T.astype(BF16)
        u = lax.broadcasted_iota(jnp.int32, (96, 384), 0)
        pose = (u & 15) * 24 + (u >> 4) * 4
        k = lax.broadcasted_iota(jnp.int32, (96, 384), 1)
        for j in range(4):
            put = jnp.where(k == pose + j, 1.0, 0.0).astype(BF16)
            part = jnp.dot(turned[j * 32 : j * 32 + 32, :], put, preferred_element_type=F32)
            part = part * float(scale)
            ids = part if ids is None else ids + part
    seg[...] = ids.astype(jnp.int32)


def route_call(h):
    return pl.pallas_call(
        route_kernel,
        in_specs=[pl.BlockSpec(memory_space=pltpu.VMEM)],
        out_specs=pl.BlockSpec(memory_space=pltpu.VMEM),
        out_shape=pltpu.VMEM((NBLK, 384), jnp.int32),
        compiler_params=LIMIT,
        cost_estimate=pl.CostEstimate(flops=1 << 26, bytes_accessed=1 << 20, transcendentals=0),
        name="route",
    )(h)


def gather_kernel(pos, pieces, e, e2, w, w2, seg, g_out, ev_out, num_out, post, post2, acc):
    step = pl.program_id(0)

    @pl.when(step == 0)
    def _():
        imgs = pieces.shape[2]
        for side, (mass, out) in enumerate(((e, post), (e2, post2))):
            group = []
            for j in range(8):
                far = jnp.bitwise_xor(pos[3], j)
                hops = jnp.right_shift(far, 1)
                hops = jnp.bitwise_xor(hops, jnp.right_shift(hops, 1))
                group.append(pieces[hops * 4 + jnp.bitwise_and(far, 1) * 2 + side])
            peak = group[0][0:1, :]
            for g in group[1:]:
                peak = jnp.maximum(peak, g[0:1, :])
            total = jnp.zeros_like(peak)
            number = jnp.zeros_like(peak)
            for g in group:
                total = total + g[1:2, :] * jnp.exp(g[0:1, :] - peak)
                number = number + g[2:3, :]
            if side == 0:
                ev_out[...] = peak + jnp.log(total)
                here = lax.broadcasted_iota(jnp.int32, number.shape, 1) == pos[4]
                num_out[...] = jnp.sum(jnp.where(here, number, 0.0), axis=1, keepdims=True)
            scale = jnp.exp(pieces[side, 0:1, :] - peak) / total
            for t in range(TRANS):
                at = slice(t * imgs, (t + 1) * imgs)
                out[:, at] = (mass[:, at] * scale).astype(BF16)
        acc[...] = jnp.zeros(acc.shape, F32)

    added = None
    for u in range(2):
        near = 2 * step + u
        at = pos[2] * w2.shape[0] + near
        rows = jnp.dot(post[...], w[at], preferred_element_type=F32)
        rows = rows + jnp.dot(post2[...], w2[near], preferred_element_type=F32)
        rows = rows.astype(BF16)
        both = jnp.concatenate([rows[:, :256], rows[:, 256:]], axis=0)
        ids = jnp.concatenate([seg[pl.ds(2 * at, 1), :], seg[pl.ds(2 * at + 1, 1), :]], axis=1)
        hot = lax.broadcasted_iota(jnp.int32, (acc.shape[0], ids.shape[1]), 0) == ids
        hot = jnp.where(hot, 1.0, 0.0).astype(BF16)
        part = jnp.dot(hot, both, preferred_element_type=F32)
        added = part if added is None else added + part
    acc[...] += added

    @pl.when(step == pl.num_programs(0) - 1)
    def _():
        g_out[...] = acc[...].astype(BF16)


def gather_call(where, pieces, e, e2, weighted, half, seg):
    segs = BRICKS * STENCILS
    vmem = pl.BlockSpec(memory_space=pltpu.VMEM)
    return pl.pallas_call(
        gather_kernel,
        grid=(half.shape[0] // 2,),
        in_specs=[pl.BlockSpec(memory_space=pltpu.SMEM)] + [vmem] * 6,
        out_specs=[vmem] * 3,
        out_shape=[
            jax.ShapeDtypeStruct((segs, 256), BF16),
            jax.ShapeDtypeStruct((1, pieces.shape[2]), F32),
            jax.ShapeDtypeStruct((1, 1), F32),
        ],
        scratch_shapes=[
            pltpu.VMEM(e.shape, BF16),
            pltpu.VMEM(e.shape, BF16),
            pltpu.VMEM((segs, 256), F32),
        ],
        compiler_params=LIMIT,
        name="gather",
    )(where, pieces, e, e2, weighted, half, seg)


def volume_kernel(got, interp, count, out):
    total = got[0].astype(F32)
    for j in range(1, got.shape[0]):
        total = total + got[j].astype(F32)
    mixed = total.astype(BF16)
    acc = jnp.zeros((STENCILS, CELLS), F32)
    for s in range(STENCILS):
        row = lax.broadcasted_iota(jnp.int32, mixed.shape, 0) == s
        only = jnp.where(row, total, 0.0).astype(BF16)
        acc = acc + jnp.dot(only, interp[0, s], preferred_element_type=F32)
    del mixed
    out[...] = jnp.sum(acc, axis=0, keepdims=True) * lax.rsqrt(1.0 + count[...])


def volume_call(got, interp, count):
    return pl.pallas_call(
        volume_kernel,
        out_shape=jax.ShapeDtypeStruct((1, CELLS), F32),
        compiler_params=LIMIT,
        name="volume",
    )(got, interp, count)


def shifted(x, axis, by):
    size = lax.axis_size(axis)
    return lax.ppermute(x, axis, [(i, (i + by) % size) for i in range(size)])


def flipped(x, axis):
    return lax.ppermute(x, axis, [(0, 1), (1, 0)])


def body(images, shift_phase, noise_weight, refs, routing, stencil, interp):
    xh, y, c = (lax.axis_index(a) for a in IMG)

    pose = lax.axis_index(POSE)
    where = jnp.stack([xh, y, c, pose, lax.axis_index(IMG_POSE)]).astype(jnp.int32)
    noise = noise_weight.reshape(16, 1, SLICE)
    mine = slice_call(where, refs, noise, routing.reshape(1, -1), stencil)

    by_block = noise_weight.reshape(1, NBLK, 2, BLOCK)
    angles = shift_phase.reshape(TRANS, NBLK, 1, BLOCK)
    cos = (jnp.cos(angles) * by_block).reshape(TRANS, 2 * PIX)
    sign = jnp.array([1.0, -1.0], F32).reshape(1, 1, 2, 1)
    sin = (jnp.sin(angles) * by_block * sign).reshape(TRANS, 2 * PIX)

    def swapped(piece):
        return flipped(piece, "c")

    near = swapped(mine)
    left = shifted(mine, "y", 1)
    right = shifted(mine, "y", -1)
    across = flipped(mine, "xh")
    other_images = swapped(images)
    weighted = weight_rows(images, cos, sin)
    one = scores_call([(mine, near, 0, 384, (0, 0))], where, weighted, None, False)
    left, weighted = lax.optimization_barrier((left, weighted))
    aleft = flipped(left, "xh")
    far = shifted(left, "y", 1)
    aright = shifted(across, "y", -1)

    def pair(piece, flips):
        return (piece, swapped(piece), 0, 384, flips)

    two = scores_call(
        [pair(left, (0, -1)), pair(right, (0, 1)), pair(across, (1, 0))],
        where, weighted, one, False,
    )
    aleft, two = lax.optimization_barrier((aleft, two))
    alow = shifted(aleft[:LOW], "y", 1)
    three = scores_call([pair(aleft, (1, -1))], where, weighted, two, False)
    aright, three = lax.optimization_barrier((aright, three))
    ahigh = shifted(aright[LOW:], "y", -1)
    four = scores_call([pair(far, (0, 2))], where, weighted, three, False)
    five = scores_call([pair(aright, (1, 1))], where, weighted, four, False)
    alow, ahigh, five = lax.optimization_barrier((alow, ahigh, five))
    low, high = swapped(alow), swapped(ahigh)
    six = scores_call(
        [(alow, None, 0, LOW, (1, 2)), (ahigh, None, LOW, 384 - LOW, (1, 2))],
        where, weighted, five, False,
    )
    marks, e, pieces = scores_call(
        [(None, low, 0, LOW, (1, 2)), (None, high, LOW, 384 - LOW, (1, 2))],
        where, weighted, six, True,
    )

    other = swapped(pieces)
    e2 = swapped(e)
    pieces = jnp.concatenate([pieces, other], axis=0)
    pieces, other_images = lax.optimization_barrier((pieces, other_images))
    half = weight_half(where, other_images, cos, sin, 0)
    for axis, bit in (("xl", 1), ("z", 1), ("z", 3)):
        size = lax.axis_size(axis)
        other = lax.ppermute(pieces, axis, [(i, i ^ bit) for i in range(size)])
        pieces = jnp.concatenate([pieces, other], axis=0)
        if axis == "xl":
            pieces, half = lax.optimization_barrier((pieces, half))
            half = weight_half(where, other_images, cos, sin, 1, half)
        elif bit == 1:
            pieces, half = lax.optimization_barrier((pieces, half))
    seg = route_call(marks)
    gathered, evidence, count = gather_call(where, pieces, e, e2, weighted, half, seg)
    got = lax.all_to_all(
        gathered.reshape(BRICKS, STENCILS, 2 * BLOCK), IMG_POSE, 0, 0, tiled=True
    )
    volume = volume_call(got, interp, count)
    return (volume, evidence.reshape(-1))


def solution(mesh):
    finer = Mesh(mesh.devices.reshape(2, 4, 2, 4, 2), ("xh", "y", "c", "z", "xl"))
    return jax.shard_map(
        body,
        mesh=finer,
        in_specs=(
            P(IMG, None),
            P(),
            P(),
            P(POSE, IMG),
            P(POSE_IMG, None),
            P(POSE_IMG),
            P(IMG_POSE, None, None, None),
        ),
        out_specs=(P(IMG_POSE, None), P(IMG)),
        check_vma=False,
    )
```

```python
import jax
import jax.numpy as jnp
from jax import lax
from jax.experimental import pallas as pl
from jax.experimental.pallas import tpu as pltpu
from jax.sharding import Mesh
from jax.sharding import PartitionSpec as P

PIX = 4096
TRANS = 8
BLOCK = 128
STENCILS = 8
NBLK = 32
BRICKS = 128
CELLS = 512
SLICE = 512
IMG = ("xh", "y", "c")
POSE = ("z", "xl")
IMG_POSE = ("xh", "y", "c", "z", "xl")
POSE_IMG = ("z", "xl", "xh", "y", "c")
F32 = jnp.float32
BF16 = jnp.bfloat16


LIMIT = pltpu.CompilerParams(vmem_limit_bytes=12 << 20)
IDS = 8
LOW = 224


def slice_kernel(pos, *arrays):
    sources, out, copied, done = arrays[:4], arrays[4], arrays[5:8], arrays[8]
    n = sources[0].shape[0]
    places = (out.at[pl.ds(0, n), :], *copied)
    copies = [
        pltpu.make_async_copy(sources[j], places[j], done.at[j]) for j in range(4)
    ]
    for copy in copies:
        copy.start()
    noise, routing, stencil = copied
    copies[2].wait()
    copies[3].wait()
    bricks = routing[...].astype(F32)
    kinds = stencil[...].reshape(1, -1).astype(F32)
    one = bricks[:, :512]
    two = jnp.concatenate([bricks[:, 512:], kinds[:, :256]], axis=1)
    three = kinds[:, 256:]
    lane = lax.broadcasted_iota(jnp.int32, (BRICKS, 128), 0)
    hits = jnp.zeros((BRICKS, 128), F32)
    for u in range(6):
        hits = hits + jnp.where(lane == routing[:, u * 128 : u * 128 + 128], 1.0, 0.0)
    counts = jnp.sum(hits.T, axis=0, keepdims=True)
    chip = pos[0] * 4 + pos[1]
    copies[0].wait()
    copies[1].wait()
    wide = out[:n, :].astype(F32)
    q = wide * wide * noise[chip * 2 + pos[2]]
    q = q[:, :128] + q[:, 128:256] + (q[:, 256:384] + q[:, 384:])
    norm = jnp.concatenate(
        [jnp.sum(q[j : j + 128, :].T, axis=0, keepdims=True) for j in range(0, n, 128)], axis=1
    )
    high = norm.astype(BF16).astype(F32)
    four = jnp.concatenate([counts, high], axis=1)
    five = jnp.concatenate([jnp.zeros_like(counts), norm - high], axis=1)
    rest = jnp.zeros((IDS - 5, SLICE), F32)
    tags = jnp.concatenate([one, two, three, four, five, rest], axis=0)
    out[n : n + IDS, :] = tags.astype(BF16)


def slice_call(where, refs, noise, routing, stencil):
    arrays = [
        pltpu.with_memory_space_constraint(a, pltpu.HBM)
        for a in (refs, noise, routing, stencil)
    ]
    return pl.pallas_call(
        slice_kernel,
        in_specs=[pl.BlockSpec(memory_space=pltpu.SMEM)]
        + [pl.BlockSpec(memory_space=pltpu.HBM)] * 4,
        out_specs=pl.BlockSpec(memory_space=pltpu.VMEM),
        scratch_shapes=[pltpu.VMEM(a.shape, a.dtype) for a in arrays[1:]]
        + [pltpu.SemaphoreType.DMA((4,))],
        out_shape=jax.ShapeDtypeStruct((refs.shape[0] + IDS, SLICE), BF16),
        compiler_params=LIMIT,
        name="slice",
    )(where, *arrays)


def weight_kernel(img, cos, sin, out, first=0):
    step = first + pl.program_id(0)
    n = img.shape[0]
    for p in range(SLICE // 256):
        re_at = slice(p * 256, p * 256 + 128)
        im_at = slice(p * 256 + 128, p * 256 + 256)
        for g in range(0, n, 16):
            re = img[g : g + 16, re_at].astype(F32)
            im = img[g : g + 16, im_at].astype(F32)
            for t in range(TRANS):
                rows = slice(t * n + g, t * n + g + 16)
                new_re = re * cos[t : t + 1, re_at] + im * sin[t : t + 1, re_at]
                new_im = im * cos[t : t + 1, im_at] + re * sin[t : t + 1, im_at]
                out[step, rows, re_at] = new_re.astype(BF16)
                out[step, rows, im_at] = new_im.astype(BF16)


def weight_rows(images, cos, sin):
    n, width = images.shape
    slices = width // SLICE
    return pl.pallas_call(
        weight_kernel,
        grid=(slices,),
        in_specs=[
            pl.BlockSpec((n, SLICE), lambda i: (0, i)),
            pl.BlockSpec((TRANS, SLICE), lambda i: (0, i)),
            pl.BlockSpec((TRANS, SLICE), lambda i: (0, i)),
        ],
        out_specs=pl.BlockSpec(memory_space=pltpu.VMEM),
        out_shape=pltpu.VMEM((slices, n * TRANS, SLICE), BF16),
        compiler_params=LIMIT,
        cost_estimate=pl.CostEstimate(flops=0, bytes_accessed=16 << 20, transcendentals=0),
        name="weigh",
    )(images, cos, sin)


def weight_half(where, images, cos, sin, turn, filled=None):
    n, width = images.shape
    slices = width // SLICE // 2
    first = turn * slices // 2

    def kernel(pos, img, cos, sin, *rest):
        weight_kernel(img, cos, sin, rest[-1], first)

    def at(i, pos):
        return (0, pos[2] * slices + first + i)

    specs = [
        pl.BlockSpec((n, SLICE), at),
        pl.BlockSpec((TRANS, SLICE), at),
        pl.BlockSpec((TRANS, SLICE), at),
    ]
    args = [where, images, cos, sin]
    vmem = pl.BlockSpec(memory_space=pltpu.VMEM)
    if filled is not None:
        specs.append(vmem)
        args.append(filled)
    return pl.pallas_call(
        kernel,
        grid_spec=pltpu.PrefetchScalarGridSpec(
            num_scalar_prefetch=1, grid=(slices // 2,), in_specs=specs, out_specs=vmem
        ),
        out_shape=pltpu.VMEM((slices, n * TRANS, SLICE), BF16),
        input_output_aliases={} if filled is None else {4: 0},
        compiler_params=LIMIT,
        cost_estimate=pl.CostEstimate(flops=0, bytes_accessed=4 << 20, transcendentals=0),
        name="weigh_half",
    )(*args)


def scores_call(pairs, where, weighted, carried, last):
    arrays = [a for pair in pairs for a in pair[:2] if a is not None]
    count = len(arrays)
    rows = weighted.shape[1]
    imgs = rows // TRANS
    poses = 384

    def kernel(pos, *refs):
        parts = list(refs[:count])
        w = refs[count]
        rest = refs[count + 1 :]
        if carried is not None:
            s_in, p_in, n_in = rest[:3]
            rest = rest[4:]
        if last:
            h_acc, e_out, st_out, s_acc = rest
        else:
            s_acc, p_acc, n_acc, h_acc = rest
        number = jnp.zeros((1, BRICKS), F32) if carried is None else n_in[...]
        norm = jnp.zeros((1, poses), F32) if carried is None else p_in[...]
        for *both, lo, n, (fx, dy) in pairs:
            chip = jnp.bitwise_xor(pos[0], fx) * 4 + jnp.bitwise_and(pos[1] + dy + 4, 3)
            total = None
            for side in range(2):
                if both[side] is None:
                    continue
                part = parts.pop(0)
                at = chip * 2 + jnp.bitwise_xor(pos[2], side)
                a = part[:n, :]
                if lo + n == poses:
                    tag = part[n : n + IDS, :].astype(F32)
                    number = number + tag[3:4, :BRICKS]
                    norm = norm + (tag[3:4, BRICKS:] + tag[4:5, BRICKS:])
                    for u in range(12):
                        lanes = slice(u % 4 * 128, u % 4 * 128 + 128)
                        h_acc[u, pl.ds(at, 1), :] = tag[u // 4 : u // 4 + 1, lanes]
                d = lax.dot_general(
                    a, w[at], (((1,), (1,)), ((), ())), preferred_element_type=F32
                )
                total = d if total is None else total + d
            at = slice(lo, lo + n)
            if carried is None:
                s_acc[at, :] = total
            else:
                s_acc[at, :] = s_in[at, :] + total
        if not last:
            n_acc[...] = number
            p_acc[...] = norm
        if last:
            half = jnp.broadcast_to(0.5 * norm, (8, poses)).T[:, :1]
            m = None
            for t in range(TRANS):
                at = slice(t * imgs, (t + 1) * imgs)
                s = jnp.max(s_acc[:, at] - half, axis=0, keepdims=True)
                m = s if m is None else jnp.maximum(m, s)
            total = jnp.zeros((1, imgs), F32)
            for t in range(TRANS):
                at = slice(t * imgs, (t + 1) * imgs)
                e = jnp.exp((s_acc[:, at] - half) - m)
                e_out[:, at] = e
                total = total + jnp.sum(e, axis=0, keepdims=True)
            st_out[0, 0:1, :] = m
            st_out[0, 1:2, :] = total
            st_out[0, 2:3, :] = number

    vmem = pl.BlockSpec(memory_space=pltpu.VMEM)
    smem = pl.BlockSpec(memory_space=pltpu.SMEM)
    in_specs = [smem] + [vmem] * (count + 1)
    args = [where, *arrays, weighted]
    acc_shapes = ((poses, rows), (1, poses), (1, BRICKS), (12, 16, 128))
    alias = {}
    if carried is not None:
        in_specs += [vmem] * 4
        alias = {len(args) + 3: 0} if last else {len(args) + j: j for j in range(4)}
        args += list(carried)
    if last:
        out_shape = [
            pltpu.VMEM(acc_shapes[3], F32),
            pltpu.VMEM((poses, rows), F32),
            jax.ShapeDtypeStruct((1, 3, imgs), F32),
        ]
        scratch = [pltpu.VMEM(acc_shapes[0], F32)]
    else:
        out_shape = [pltpu.VMEM(s, F32) for s in acc_shapes]
        scratch = []
    work = sum(2 * 2 * p[3] * SLICE * rows for p in pairs)
    return pl.pallas_call(
        kernel,
        in_specs=in_specs,
        out_specs=[vmem] * len(out_shape),
        scratch_shapes=scratch,
        out_shape=out_shape,
        input_output_aliases=alias,
        compiler_params=LIMIT,
        cost_estimate=pl.CostEstimate(flops=work, bytes_accessed=1 << 20, transcendentals=0),
        name="scores",
    )(*args)


def route_kernel(pos, h, seg):
    ids = None
    for kind, scale in ((0, STENCILS), (1, 1)):
        flat = h[6 * kind : 6 * kind + 6].reshape(96, 128)
        turned = flat.T.astype(BF16)
        u = lax.broadcasted_iota(jnp.int32, (96, 384), 0)
        pose = (u & 15) * 24 + (u >> 4) * 4
        k = lax.broadcasted_iota(jnp.int32, (96, 384), 1)
        for j in range(4):
            put = jnp.where(k == pose + j, 1.0, 0.0).astype(BF16)
            part = jnp.dot(turned[j * 32 : j * 32 + 32, :], put, preferred_element_type=F32)
            part = part * float(scale)
            ids = part if ids is None else ids + part
    ids = ids.astype(jnp.int32)
    core = jnp.bitwise_and(jnp.right_shift(ids, 6), 1)
    short = jnp.right_shift(ids, 7) * 64 + jnp.bitwise_and(ids, 63)
    seg[0] = jnp.where(core == pos[2], -1, short)
    seg[1] = jnp.where(core == pos[2], short, -1)


def route_call(where, h):
    return pl.pallas_call(
        route_kernel,
        in_specs=[
            pl.BlockSpec(memory_space=pltpu.SMEM),
            pl.BlockSpec(memory_space=pltpu.VMEM),
        ],
        out_specs=pl.BlockSpec(memory_space=pltpu.VMEM),
        out_shape=pltpu.VMEM((2, NBLK, 384), jnp.int32),
        compiler_params=LIMIT,
        cost_estimate=pl.CostEstimate(flops=1 << 26, bytes_accessed=1 << 20, transcendentals=0),
        name="route",
    )(where, h)


def picked(seg, side, at, rows, count):
    ids = [seg[side, pl.ds(2 * at + j, 1), :] for j in range(2)]
    hot = lax.broadcasted_iota(jnp.int32, (count, 768), 0) == jnp.concatenate(ids, axis=1)
    hot = jnp.where(hot, 1.0, 0.0).astype(BF16)
    return jnp.dot(hot, rows, preferred_element_type=F32)


def gather_kernel(
    pos, pieces, e, e2, w, w2, seg, g_out, store, ev_out, num_out, post, post2, acc
):
    step = pl.program_id(0)

    @pl.when(step == 0)
    def _():
        imgs = pieces.shape[2]
        for side, (mass, out) in enumerate(((e, post), (e2, post2))):
            group = []
            for j in range(8):
                far = jnp.bitwise_xor(pos[3], j)
                hops = jnp.right_shift(far, 1)
                hops = jnp.bitwise_xor(hops, jnp.right_shift(hops, 1))
                group.append(pieces[hops * 4 + jnp.bitwise_and(far, 1) * 2 + side])
            peak = group[0][0:1, :]
            for g in group[1:]:
                peak = jnp.maximum(peak, g[0:1, :])
            total = jnp.zeros_like(peak)
            number = jnp.zeros_like(peak)
            for g in group:
                total = total + g[1:2, :] * jnp.exp(g[0:1, :] - peak)
                number = number + g[2:3, :]
            if side == 0:
                ev_out[...] = peak + jnp.log(total)
                here = lax.broadcasted_iota(jnp.int32, number.shape, 1) == pos[4]
                num_out[...] = jnp.sum(jnp.where(here, number, 0.0), axis=1, keepdims=True)
            scale = jnp.exp(pieces[side, 0:1, :] - peak) / total
            for t in range(TRANS):
                at = slice(t * imgs, (t + 1) * imgs)
                out[:, at] = (mass[:, at] * scale).astype(BF16)
        acc[...] = jnp.zeros(acc.shape, F32)

    added = None
    for u in range(2):
        near = 2 * step + u
        at = pos[2] * w2.shape[0] + near
        rows = jnp.dot(post[...], w[at], preferred_element_type=F32)
        rows = rows + jnp.dot(post2[...], w2[near], preferred_element_type=F32)
        rows = rows.astype(BF16)
        both = jnp.concatenate([rows[:, :256], rows[:, 256:]], axis=0)
        store[near] = both
        part = picked(seg, 0, at, both, acc.shape[0])
        added = part if added is None else added + part
    acc[...] += added

    @pl.when(step == pl.num_programs(0) - 1)
    def _():
        g_out[...] = acc[...].astype(BF16)


def gather_call(where, pieces, e, e2, weighted, half, seg):
    segs = BRICKS * STENCILS // 2
    vmem = pl.BlockSpec(memory_space=pltpu.VMEM)
    return pl.pallas_call(
        gather_kernel,
        grid=(half.shape[0] // 2,),
        in_specs=[pl.BlockSpec(memory_space=pltpu.SMEM)] + [vmem] * 6,
        out_specs=[vmem] * 4,
        out_shape=[
            jax.ShapeDtypeStruct((segs, 256), BF16),
            pltpu.VMEM((half.shape[0], 768, 256), BF16),
            jax.ShapeDtypeStruct((1, pieces.shape[2]), F32),
            jax.ShapeDtypeStruct((1, 1), F32),
        ],
        scratch_shapes=[
            pltpu.VMEM(e.shape, BF16),
            pltpu.VMEM(e.shape, BF16),
            pltpu.VMEM((segs, 256), F32),
        ],
        compiler_params=LIMIT,
        cost_estimate=pl.CostEstimate(flops=1 << 33, bytes_accessed=1 << 20, transcendentals=0),
        name="gather",
    )(where, pieces, e, e2, weighted, half, seg)


def keep_kernel(pos, store, seg, out):
    total = None
    for near in range(store.shape[0]):
        at = pos[2] * store.shape[0] + near
        part = picked(seg, 1, at, store[near], out.shape[0])
        total = part if total is None else total + part
    out[...] = total


def keep_call(where, store, seg):
    vmem = pl.BlockSpec(memory_space=pltpu.VMEM)
    return pl.pallas_call(
        keep_kernel,
        in_specs=[pl.BlockSpec(memory_space=pltpu.SMEM)] + [vmem] * 2,
        out_specs=vmem,
        out_shape=pltpu.VMEM((BRICKS * STENCILS // 2, 256), F32),
        compiler_params=LIMIT,
        cost_estimate=pl.CostEstimate(flops=1 << 31, bytes_accessed=1 << 20, transcendentals=0),
        name="keep",
    )(where, store, seg)


def volume_kernel(got, interp, count, out):
    total = got[0].astype(F32)
    for j in range(1, got.shape[0]):
        total = total + got[j].astype(F32)
    mixed = total.astype(BF16)
    acc = jnp.zeros((STENCILS, CELLS), F32)
    for s in range(STENCILS):
        row = lax.broadcasted_iota(jnp.int32, mixed.shape, 0) == s
        only = jnp.where(row, total, 0.0).astype(BF16)
        acc = acc + jnp.dot(only, interp[0, s], preferred_element_type=F32)
    del mixed
    out[...] = jnp.sum(acc, axis=0, keepdims=True) * lax.rsqrt(1.0 + count[...])


def volume_call(got, interp, count):
    return pl.pallas_call(
        volume_kernel,
        out_shape=jax.ShapeDtypeStruct((1, CELLS), F32),
        compiler_params=LIMIT,
        name="volume",
    )(got, interp, count)


def shifted(x, axis, by):
    size = lax.axis_size(axis)
    return lax.ppermute(x, axis, [(i, (i + by) % size) for i in range(size)])


def flipped(x, axis):
    return lax.ppermute(x, axis, [(0, 1), (1, 0)])


def body(images, shift_phase, noise_weight, refs, routing, stencil, interp):
    xh, y, c = (lax.axis_index(a) for a in IMG)

    pose = lax.axis_index(POSE)
    where = jnp.stack([xh, y, c, pose, lax.axis_index(IMG_POSE)]).astype(jnp.int32)
    noise = noise_weight.reshape(16, 1, SLICE)
    mine = slice_call(where, refs, noise, routing.reshape(1, -1), stencil)

    by_block = noise_weight.reshape(1, NBLK, 2, BLOCK)
    angles = shift_phase.reshape(TRANS, NBLK, 1, BLOCK)
    cos = (jnp.cos(angles) * by_block).reshape(TRANS, 2 * PIX)
    sign = jnp.array([1.0, -1.0], F32).reshape(1, 1, 2, 1)
    sin = (jnp.sin(angles) * by_block * sign).reshape(TRANS, 2 * PIX)

    def swapped(piece):
        return flipped(piece, "c")

    near = swapped(mine)
    left = shifted(mine, "y", 1)
    right = shifted(mine, "y", -1)
    across = flipped(mine, "xh")
    other_images = swapped(images)
    weighted = weight_rows(images, cos, sin)
    one = scores_call([(mine, near, 0, 384, (0, 0))], where, weighted, None, False)
    left, weighted = lax.optimization_barrier((left, weighted))
    aleft = flipped(left, "xh")
    far = shifted(left, "y", 1)
    aright = shifted(across, "y", -1)

    def pair(piece, flips):
        return (piece, swapped(piece), 0, 384, flips)

    two = scores_call(
        [pair(left, (0, -1)), pair(right, (0, 1)), pair(across, (1, 0))],
        where, weighted, one, False,
    )
    aleft, two = lax.optimization_barrier((aleft, two))
    alow = shifted(aleft[:LOW], "y", 1)
    ahigh = shifted(aright[LOW:], "y", -1)
    three = scores_call([pair(aleft, (1, -1))], where, weighted, two, False)
    four = scores_call([pair(far, (0, 2))], where, weighted, three, False)
    five = scores_call([pair(aright, (1, 1))], where, weighted, four, False)
    alow, ahigh, five = lax.optimization_barrier((alow, ahigh, five))
    low, high = swapped(alow), swapped(ahigh)
    six = scores_call(
        [(alow, None, 0, LOW, (1, 2)), (ahigh, None, LOW, 384 - LOW, (1, 2))],
        where, weighted, five, False,
    )
    marks, e, pieces = scores_call(
        [(None, low, 0, LOW, (1, 2)), (None, high, LOW, 384 - LOW, (1, 2))],
        where, weighted, six, True,
    )

    other = swapped(pieces)
    e2 = swapped(e)
    pieces = jnp.concatenate([pieces, other], axis=0)
    pieces, other_images = lax.optimization_barrier((pieces, other_images))
    half = weight_half(where, other_images, cos, sin, 0)
    for axis, bit in (("xl", 1), ("z", 1), ("z", 3)):
        size = lax.axis_size(axis)
        other = lax.ppermute(pieces, axis, [(i, i ^ bit) for i in range(size)])
        pieces = jnp.concatenate([pieces, other], axis=0)
        if axis == "xl":
            pieces, half = lax.optimization_barrier((pieces, half))
            half = weight_half(where, other_images, cos, sin, 1, half)
        elif bit == 1:
            pieces, half = lax.optimization_barrier((pieces, half))
    seg = route_call(where, marks)
    given, store, evidence, count = gather_call(where, pieces, e, e2, weighted, half, seg)
    taken = swapped(given)
    kept = keep_call(where, store, seg)
    gathered = (kept + taken.astype(F32)).astype(BF16)
    got = lax.all_to_all(
        gathered.reshape(BRICKS // 2, STENCILS, 2 * BLOCK),
        ("xh", "y", "z", "xl"), 0, 0, tiled=True,
    )
    volume = volume_call(got, interp, count)
    return (volume, evidence.reshape(-1))


def solution(mesh):
    finer = Mesh(mesh.devices.reshape(2, 4, 2, 4, 2), ("xh", "y", "c", "z", "xl"))
    return jax.shard_map(
        body,
        mesh=finer,
        in_specs=(
            P(IMG, None),
            P(),
            P(),
            P(POSE, IMG),
            P(POSE_IMG, None),
            P(POSE_IMG),
            P(IMG_POSE, None, None, None),
        ),
        out_specs=(P(IMG_POSE, None), P(IMG)),
        check_vma=False,
    )
```
